32 devices in a mesh: context: 8 (over z, x), tensor: 4 (over y, core).
Axes of the slice: x: 2, y: 2, z: 4, core: 2. Of those that a mesh axis runs over, the one named last changes fastest.
Arguments:
- length: int32 [1], replicated, may hold values from 512 to 1024
- mamba_in: bfloat16 [1024, 8192], P('context', 'tensor'), may hold values from -6 to 6
- gate_in: bfloat16 [1024, 8192], P('context', 'tensor'), may hold values from -6 to 6
- step_raw: bfloat16 [1024, 8192], P('context', 'tensor'), may hold values from -3 to 3
- conv_weight: float32 [4, 8192], P(None, 'tensor'), may hold values from -3 to 3
- conv_bias: float32 [8192], P('tensor'), may hold values from -3 to 3
- step_bias: float32 [8192], P('tensor'), may hold values from -1 to 1
- decay_rates: float32 [16, 8192], P(None, 'tensor'), may hold values from 4.8828126e-05 to 0.04
- skip_gain: float32 [8192], P('tensor'), may hold values from 0.5 to 1.5
- state_proj: bfloat16 [8192, 32], P('tensor'), may hold values from -0.015625 to 0.015625
- query_input_rows: bfloat16 [1024, 4096], P('context', 'tensor'), may hold values from -113.60155108391487 to 113.60155108391487
- key_input_rows: bfloat16 [1024, 512], P('context', 'tensor'), may hold values from -4 to 4
- value_input_rows: bfloat16 [1024, 512], P('context', 'tensor'), may hold values from -6 to 6
Outputs:
- mamba_out: bfloat16 [1024, 8192], P('context', 'tensor')
- attn_out: bfloat16 [1024, 4096], P('context', 'tensor')
The draws below stay inside these ranges and needn't reach their ends.
All inputs are finite; a program needn't handle non-finite values.
Results may differ from the reference program's by a relative error of at most 0.0085.
Values may be sent and summed in bfloat16 or wider, within the bound.
A program may use at most 128 MiB of HBM per device.

```python
import math
import jax
import jax.numpy as jnp
from jax import lax

DI = 8192
NS = 16
KW = 4
HEAD_WIDTH = 128
QUERY_HEADS = 32
KEY_VALUE_HEADS = 4
PROMPT_TOKENS = 1024


def key_head_table(key):
    base_offset = jax.random.normal(jax.random.fold_in(key, 11), (PROMPT_TOKENS, KEY_VALUE_HEADS * HEAD_WIDTH), jnp.float32)
    return jnp.clip(base_offset, -4.0, 4.0)


def draw_key_input_rows(key, part):
    return key_head_table(key).astype(jnp.bfloat16)


def draw_query_input_rows(key, part):
    base_offset = jax.random.normal(jax.random.fold_in(key, 23), (PROMPT_TOKENS, QUERY_HEADS * HEAD_WIDTH), jnp.float32)
    base_offset = jnp.clip(base_offset, -4.0, 4.0)
    return base_offset.astype(jnp.bfloat16)


def levels(stream_key, shape, split, least, largest):
    factor_of, own = 1.0, jax.random.fold_in(stream_key, 6)
    for dim, shards_of in split:
        draws = jnp.exp(jax.random.uniform(jax.random.fold_in(own, dim), (shards_of,), jnp.float32, least / len(split), largest / len(split)))
        factor_of = factor_of * jnp.repeat(draws, shape[dim] // shards_of).reshape([-1 if axis == dim else 1 for axis in range(len(shape))])
    return factor_of


def gaussian(rng, extent, spread, limit, cuts=(), kind=jnp.bfloat16):
    drawn = jax.random.normal(rng, extent, jnp.float32) * spread
    if len(cuts) > 0:
        drawn = levels(rng, extent, cuts, -0.22, 0.18) * drawn
    return jnp.clip(drawn, min=-limit, max=limit).astype(kind)


def setup_inputs(seed: int = 0) -> dict:
    keys = jax.random.split(jax.random.key(seed), 14)
    length = jax.random.randint(keys[0], (1,), PROMPT_TOKENS // 2, PROMPT_TOKENS + 1).astype(jnp.int32)
    mamba_in = gaussian(keys[1], (PROMPT_TOKENS, DI), 1.0, 6.0, ((0, 8), (1, 4)))
    gate_in = gaussian(keys[2], (PROMPT_TOKENS, DI), 1.0, 6.0, ((0, 8), (1, 4)))
    step_raw = gaussian(keys[3], (PROMPT_TOKENS, DI), 0.5, 3.0, ((0, 8), (1, 4)))
    conv_weight = gaussian(keys[4], (KW, DI), KW ** -0.5, 3.0, ((1, 4),), jnp.float32)
    conv_bias = gaussian(keys[5], (DI,), 0.5, 3.0, ((0, 4),), jnp.float32)
    step_bias = jnp.clip(jax.random.uniform(keys[6], (DI,), jnp.float32, -1.0, 1.0) * levels(keys[6], (DI,), ((0, 4),), -0.4, 0.0), -1.0, 1.0)
    decay_rates = jnp.clip(jnp.exp(math.log(0.04) - 6.7083282 * jax.random.uniform(keys[7], (NS, DI), jnp.float32) ** levels(keys[7], (NS, DI), ((1, 4),), -0.2, 0.2)), 4.882812572759576e-05, 0.04)
    skip_gain = jnp.clip(0.5 + 1.0 * jax.random.uniform(keys[8], (DI,), jnp.float32) ** levels(keys[8], (DI,), ((0, 4),), -0.2, 0.2), 0.5, 1.5)
    state_proj = gaussian(keys[9], (DI, 2 * NS), (DI * PROMPT_TOKENS // 64) ** -0.5, 0.015625, ((0, 4),))
    query_input_rows = draw_query_input_rows(jax.random.fold_in(keys[13], 71), 0)
    key_input_rows = draw_key_input_rows(jax.random.fold_in(keys[13], 71), 0)
    value_input_rows = gaussian(keys[12], (PROMPT_TOKENS, KEY_VALUE_HEADS * HEAD_WIDTH), 1.0, 6.0, ((0, 8), (1, 4)))
    return {"length": length, "mamba_in": mamba_in, "gate_in": gate_in, "step_raw": step_raw, "conv_weight": conv_weight, "conv_bias": conv_bias, "step_bias": step_bias, "decay_rates": decay_rates, "skip_gain": skip_gain, "state_proj": state_proj, "query_input_rows": query_input_rows, "key_input_rows": key_input_rows, "value_input_rows": value_input_rows}


def mamba_part(length, mamba_in, gate_in, step_raw, conv_weight, conv_bias, step_bias, decay_rates, skip_gain, state_proj):
    input_float = mamba_in.astype(jnp.float32)
    padded = jnp.concatenate([jnp.zeros((KW - 1, DI), jnp.float32), input_float], axis=0)
    convolved = jnp.broadcast_to(conv_bias[None, :], input_float.shape)
    for tap_index in range(KW):
        convolved = convolved + conv_weight[tap_index][None, :] * padded[tap_index:tap_index + PROMPT_TOKENS]
    conv_out = jax.nn.silu(convolved).astype(jnp.bfloat16)
    projected = jnp.dot(conv_out, state_proj, preferred_element_type=jnp.float32)
    inject = projected[:, :NS]
    readout = projected[:, NS:]
    positions = jnp.arange(PROMPT_TOKENS, dtype=jnp.int32)
    is_valid = (positions < length[0]).astype(jnp.float32)
    step_size = jax.nn.softplus(step_raw.astype(jnp.float32) + step_bias[None, :]) * is_valid[:, None]
    mixed_float = conv_out.astype(jnp.float32)

    def advance(state, inputs):
        step_now, inject_now, readout_now, mixed_step = inputs
        state = jnp.exp(-decay_rates * step_now[None, :]) * state + inject_now[:, None] * (step_now * mixed_step)[None, :]
        return (state, lax.optimization_barrier(jnp.sum(readout_now[:, None] * state, axis=0)))
    _, scanned = lax.scan(advance, jnp.zeros((NS, DI), jnp.float32), (step_size, inject, readout, mixed_float))
    mixed = (scanned + skip_gain[None, :] * mixed_float) * jax.nn.silu(gate_in.astype(jnp.float32))
    return mixed.astype(jnp.bfloat16)

def attention_part(length, query_input_rows, key_input_rows, value_input_rows):
    query_group_count = QUERY_HEADS // KEY_VALUE_HEADS
    query_head_rows = query_input_rows.reshape(PROMPT_TOKENS, KEY_VALUE_HEADS, query_group_count, HEAD_WIDTH)
    key_head_rows = key_input_rows.reshape(PROMPT_TOKENS, KEY_VALUE_HEADS, HEAD_WIDTH).astype(jnp.float32)
    value_head_rows = value_input_rows.reshape(PROMPT_TOKENS, KEY_VALUE_HEADS, HEAD_WIDTH).astype(jnp.float32)
    score_scale = 1.0 / math.sqrt(HEAD_WIDTH)
    query_block = math.gcd(PROMPT_TOKENS, 128)
    positions = jnp.arange(PROMPT_TOKENS, dtype=jnp.int32)
    key_valid = positions < length[0]

    def one_block(block_index):
        start = (block_index * query_block).astype(jnp.int32)
        block_queries = lax.dynamic_slice_in_dim(query_head_rows, start, query_block, 0).astype(jnp.float32)
        scores = jnp.einsum('qhgd,khd->qhgk', block_queries, key_head_rows, precision=lax.Precision.HIGHEST) * score_scale
        query_pos = start + jnp.arange(query_block, dtype=jnp.int32)
        allowed = (positions[None, :] <= query_pos[:, None]) & key_valid[None, :]
        scores = jnp.where(allowed[:, None, None, :], scores, -jnp.inf)
        highest = lax.optimization_barrier(jnp.max(scores, axis=-1))
        weights = jnp.exp(scores - highest[..., None])
        total = lax.optimization_barrier(jnp.sum(weights, axis=-1))
        rounded = lax.optimization_barrier(weights.astype(jnp.bfloat16)).astype(jnp.float32)
        summed = jnp.einsum('qhgk,khd->qhgd', rounded, value_head_rows, precision=lax.Precision.HIGHEST)
        return (summed / total[..., None]).astype(jnp.bfloat16)
    blocks = lax.map(one_block, jnp.arange(PROMPT_TOKENS // query_block, dtype=jnp.int32))
    return blocks.reshape(PROMPT_TOKENS, QUERY_HEADS * HEAD_WIDTH)

def reference(length, mamba_in, gate_in, step_raw, conv_weight, conv_bias, step_bias, decay_rates, skip_gain, state_proj, query_input_rows, key_input_rows, value_input_rows):
    mamba_out = mamba_part(length, mamba_in, gate_in, step_raw, conv_weight, conv_bias, step_bias, decay_rates, skip_gain, state_proj)
    attn_out = attention_part(length, query_input_rows, key_input_rows, value_input_rows)
    return (mamba_out, attn_out)
```

```python
import functools
import math

import jax
import jax.numpy as jnp
from jax import lax
from jax.experimental import pallas as pl
from jax.experimental.pallas import tpu as pltpu
from jax.sharding import PartitionSpec as P

KW = 4
HEAD_WIDTH = 128
LANES = 128
LOG2E = 1.4426950408889634
LOW = -1e30
MESH = pl.DeviceIdType.MESH
F32 = jnp.float32
BF16 = jnp.bfloat16


def each(count, body):
    if count <= 8:
        for i in range(count):
            body(i)
    else:
        @pl.loop(0, count)
        def _(i):
            body(i)


def blocked(count, step, body, start=0):
    @pl.loop(start // step, count // step)
    def _(block):
        for k in range(step):
            body(block * step + k)


def silu(v):
    return v / (1.0 + jnp.exp(-v))


def kernel(
    n_ctx, n_ten, group,
    length, mamba, gate, step_raw, conv_w, conv_b, step_b, rates, skip, proj, query, keys, values,
    mamba_out, attn_out,
    x_a, conv_a, step_a, elapsed_a, gate_a, y_a, rate_a, taps_a, spread,
    part_all, e_all, s_out, s_in, p_out, p_in, inc_a, k_all, v_all, sc, top, tot, acc,
    halo_send, halo_recv, part_send, part_recv, e_send, e_recv, s_send, s_recv,
    p_send, p_recv, k_send, k_recv, v_send, v_recv,
):
    tok, chans = mamba.shape
    ch = chans // LANES
    ns = rates.shape[0]
    pieces = ns * ch // n_ctx
    me = lax.axis_index("context")
    mt = lax.axis_index("tensor")

    def ctx_copy(src, dst, send, recv, to):
        return pltpu.make_async_remote_copy(
            src_ref=src, dst_ref=dst, send_sem=send, recv_sem=recv,
            device_id={"context": to}, device_id_type=MESH,
        )

    def others(body):
        each(n_ctx - 1, lambda d: body(lax.rem(me + d + 1, n_ctx)))

    barrier = pltpu.get_barrier_semaphore()
    others(lambda to: pl.semaphore_signal(barrier, inc=1, device_id={"context": to}, device_id_type=MESH))
    for d in range(1, n_ten):
        pl.semaphore_signal(
            barrier, inc=1, device_id={"tensor": lax.rem(mt + d, n_ten)}, device_id_type=MESH
        )

    prompt_end = length[0]
    first = me * tok
    valid = (first + lax.broadcasted_iota(jnp.int32, (tok, LANES), 0)) < prompt_end
    pad = (KW - 1) * ch

    @pl.loop(0, ch)
    def _(c):
        lanes = pl.ds(pl.multiple_of(c * LANES, LANES), LANES)
        x_a[pl.ds(pad + c, tok, stride=ch), :] = mamba[:, lanes].astype(F32)
        raw = step_raw[:, lanes].astype(F32) + step_b[pl.ds(c, 1), :]
        size = jnp.maximum(raw, 0.0) + jnp.log(1.0 + jnp.exp(-jnp.abs(raw)))
        step_a[pl.ds(c, tok, stride=ch), :] = jnp.where(valid, size, 0.0)
        rate_a[pl.ds(c, ns, stride=ch), :] = rates[:, lanes] * (-LOG2E)
        for j in range(KW):
            taps_a[pl.ds(j * ch + c, 1), :] = conv_w[j : j + 1, lanes]

    pl.semaphore_wait(barrier, n_ctx - 1 + n_ten - 1)

    halo = ctx_copy(
        x_a.at[pl.ds(tok * ch, pad), :], x_a.at[pl.ds(0, pad), :],
        halo_send, halo_recv, lax.rem(me + 1, n_ctx),
    )

    @pl.when(me < n_ctx - 1)
    def _():
        halo.start()

    def kv_copies(src, to):
        return (
            ctx_copy(keys, k_all.at[src], k_send.at[to], k_recv.at[src], to),
            ctx_copy(values, v_all.at[src], v_send.at[to], v_recv.at[src], to),
        )

    def later(body):
        def visit(d):
            to = me + d + 1

            @pl.when(to < n_ctx)
            def _():
                body(to)

        each(n_ctx - 1, visit)

    def start_kv(to):
        for copy in kv_copies(me, to):
            copy.start()

    later(start_kv)
    k_all[me] = keys[...]
    v_all[me] = values[...]

    def run_elapsed(i, total):
        for k in range(4):
            rows = pl.ds(pl.multiple_of((i * 4 + k) * ch, ch), ch)
            total = total + step_a[rows, :]
            elapsed_a[rows, :] = total
        return total

    e_all[me] = lax.fori_loop(0, tok // 4, run_elapsed, jnp.zeros((ch, LANES), F32))

    def e_copy(src, to):
        return ctx_copy(e_all.at[src], e_all.at[src], e_send.at[to], e_recv.at[src], to)

    others(lambda to: e_copy(me, to).start())

    bias = conv_b[...]

    def convolve(t):
        total = bias
        for j in range(KW):
            total = total + taps_a[j * ch : (j + 1) * ch, :] * x_a[
                pl.ds(pl.multiple_of((t + j) * ch, ch), ch), :
            ]
        conv_a[pl.ds(pl.multiple_of(t * ch, ch), ch), :] = silu(total).astype(BF16).astype(F32)

    blocked(tok, 4, convolve, start=4)

    @pl.when(me > 0)
    def _():
        halo.wait_recv()

    @pl.when(me == 0)
    def _():
        x_a[0:pad, :] = jnp.zeros((pad, LANES), F32)

    for t in range(4):
        convolve(t)

    part = jnp.zeros((tok, 2 * ns), F32)
    for c in range(ch):
        part = part + jnp.dot(
            conv_a[pl.ds(c, tok, stride=ch), :].astype(BF16),
            proj[c * LANES : (c + 1) * LANES, :],
            preferred_element_type=F32,
        )
    part_all[mt] = part.T

    def part_copy(src, to):
        return pltpu.make_async_remote_copy(
            src_ref=part_all.at[src], dst_ref=part_all.at[src],
            send_sem=part_send.at[to], recv_sem=part_recv.at[src],
            device_id={"tensor": to}, device_id_type=MESH,
        )

    for d in range(1, n_ten):
        part_copy(mt, lax.rem(mt + d, n_ten)).start()

    @pl.loop(0, ch)
    def _(c):
        lanes = pl.ds(pl.multiple_of(c * LANES, LANES), LANES)
        gate_a[pl.ds(c, tok, stride=ch), :] = silu(gate[:, lanes].astype(F32))

    for d in range(1, n_ten):
        part_copy(lax.rem(mt + d, n_ten), mt).wait_recv()
    projected = part_all[0]
    for d in range(1, n_ten):
        projected = projected + part_all[d]
    projected = projected.T
    for n in range(2 * ns):
        spread[pl.ds(n, tok, stride=2 * ns), :] = jnp.broadcast_to(
            projected[:, n : n + 1], (tok, LANES)
        )

    skip_now = skip[...]

    def advance(t, states):
        rows = pl.ds(pl.multiple_of(t * ch, ch), ch)
        size = step_a[rows, :]
        mixed = conv_a[rows, :]
        driven = size * mixed
        sums = [skip_now * mixed, None]
        new = []
        for n in range(ns):
            decay = jnp.exp2(rate_a[n * ch : (n + 1) * ch, :] * size)
            inject = jnp.broadcast_to(spread[pl.ds(t * 2 * ns + n, 1), :], (ch, LANES))
            readout = jnp.broadcast_to(spread[pl.ds(t * 2 * ns + ns + n, 1), :], (ch, LANES))
            state = decay * states[n] + inject * driven
            new.append(state)
            term = readout * state
            sums[n % 2] = term if sums[n % 2] is None else sums[n % 2] + term
        y_a[rows, :] = sums[0] + sums[1]
        return tuple(new)

    finals = lax.fori_loop(
        0, tok, advance, tuple(jnp.zeros((ch, LANES), F32) for _ in range(ns))
    )
    whole_state = jnp.concatenate(finals, axis=0).astype(s_out.dtype)
    s_out[...] = whole_state.reshape(n_ctx, pieces, LANES)

    def s_copy(src, to):
        return ctx_copy(s_out.at[to], s_in.at[src], s_send.at[to], s_recv.at[src], to)

    others(lambda to: s_copy(me, to).start())
    s_in[me] = s_out[me]

    @pl.loop(0, me)
    def _(src):
        for copy in kv_copies(src, me):
            copy.wait_recv()

    scale = LOG2E / math.sqrt(HEAD_WIDTH)
    heads = query.shape[1] // HEAD_WIDTH
    row_pos = first + lax.broadcasted_iota(jnp.int32, (tok, tok), 0)
    last_key = jnp.minimum(row_pos, prompt_end - 1)
    key_iota = lax.broadcasted_iota(jnp.int32, (tok, tok), 1)

    def attend(head0):
        top[...] = jnp.full(top.shape, LOW, F32)
        tot[...] = jnp.zeros(tot.shape, F32)
        acc[...] = jnp.zeros(acc.shape, F32)

        @pl.loop(0, me + 1)
        def _(j):
            block = k_all[j]
            allowed = (key_iota + j * tok) <= last_key
            for g in range(group):
                cols = slice((head0 + g) * HEAD_WIDTH, (head0 + g + 1) * HEAD_WIDTH)
                s = lax.dot_general(
                    query[:, cols], block, (((1,), (1,)), ((), ())), preferred_element_type=F32
                )
                s = jnp.where(allowed, s, LOW)
                top[g] = jnp.maximum(top[g], s)
                sc[j, g] = s

        highest = [jnp.max(top[g], axis=1, keepdims=True) for g in range(group)]
        for g in range(group):
            top[g] = jnp.broadcast_to(highest[g], (tok, tok))

        @pl.loop(0, me + 1)
        def _(j):
            block = v_all[j]
            for g in range(group):
                w = jnp.exp2((sc[j, g] - top[g]) * scale)
                tot[g] = tot[g] + w
                acc[g] = acc[g] + jnp.dot(w.astype(BF16), block, preferred_element_type=F32)

        for g in range(group):
            cols = slice((head0 + g) * HEAD_WIDTH, (head0 + g + 1) * HEAD_WIDTH)
            total = jnp.sum(tot[g], axis=1, keepdims=True)
            attn_out[:, cols] = (acc[g] / total).astype(BF16)

    starts = list(range(0, heads, group))
    half = len(starts) // 2
    for head0 in starts[:half]:
        attend(head0)

    others(lambda src: e_copy(src, me).wait_recv())
    others(lambda src: s_copy(src, me).wait_recv())
    my_rate = rate_a[pl.ds(me * pieces, pieces), :]

    def fold(j, running):
        p_out[j] = running.astype(p_out.dtype)
        if pieces >= ch:
            gone = jnp.concatenate([e_all[j]] * (pieces // ch), axis=0)
        else:
            gone = e_all[j, pl.ds(lax.rem(me * pieces, ch), pieces), :]
        return jnp.exp2(my_rate * gone) * running + s_in[j].astype(F32)

    lax.fori_loop(0, n_ctx, fold, jnp.zeros((pieces, LANES), F32))

    def p_copy(src, to):
        return ctx_copy(p_out.at[to], p_in.at[src], p_send.at[to], p_recv.at[src], to)

    others(lambda to: p_copy(me, to).start())
    p_in[me] = p_out[me]

    for head0 in starts[half:]:
        attend(head0)

    others(lambda src: p_copy(src, me).wait_recv())
    inc_a[...] = p_in[...].reshape(ns * ch, LANES).astype(F32)

    def correct(t):
        rows = pl.ds(pl.multiple_of(t * ch, ch), ch)
        gone = elapsed_a[rows, :]
        sums = [y_a[rows, :], None]
        for n in range(ns):
            held = jnp.exp2(rate_a[n * ch : (n + 1) * ch, :] * gone) * inc_a[n * ch : (n + 1) * ch, :]
            term = jnp.broadcast_to(spread[pl.ds(t * 2 * ns + ns + n, 1), :], (ch, LANES)) * held
            sums[n % 2] = term if sums[n % 2] is None else sums[n % 2] + term
        y_a[rows, :] = (sums[0] + sums[1]) * gate_a[rows, :]

    blocked(tok, 2, correct)

    @pl.loop(0, ch)
    def _(c):
        lanes = pl.ds(pl.multiple_of(c * LANES, LANES), LANES)
        mamba_out[:, lanes] = y_a[pl.ds(c, tok, stride=ch), :].astype(BF16)

    @pl.when(me < n_ctx - 1)
    def _():
        halo.wait_send()

    def end_kv(to):
        for copy in kv_copies(me, to):
            copy.wait_send()

    later(end_kv)
    others(lambda to: e_copy(me, to).wait_send())
    others(lambda to: s_copy(me, to).wait_send())
    others(lambda to: p_copy(me, to).wait_send())
    for d in range(1, n_ten):
        part_copy(mt, lax.rem(mt + d, n_ten)).wait_send()


def shards(
    n_ctx, n_ten,
    length, mamba_in, gate_in, step_raw, conv_weight, conv_bias, step_bias, decay_rates, skip_gain,
    state_proj, query_input_rows, key_input_rows, value_input_rows,
):
    tok, chans = mamba_in.shape
    ch = chans // LANES
    ns = decay_rates.shape[0]
    heads = query_input_rows.shape[1] // HEAD_WIDTH
    group = heads // 2
    while group > 1 and n_ctx * group * tok * tok * 4 > (17 << 20):
        group //= 2
    pieces = ns * ch // n_ctx
    link = BF16 if pieces % 16 == 0 else F32
    dma = pltpu.SemaphoreType.DMA
    flat = pltpu.VMEM((tok * ch, LANES), F32)
    vmem = pl.BlockSpec(memory_space=pltpu.VMEM)
    return pl.pallas_call(
        functools.partial(kernel, n_ctx, n_ten, group),
        out_shape=(
            jax.ShapeDtypeStruct(mamba_in.shape, BF16),
            jax.ShapeDtypeStruct(query_input_rows.shape, BF16),
        ),
        in_specs=[pl.BlockSpec(memory_space=pltpu.SMEM)] + [vmem] * 12,
        out_specs=(vmem, vmem),
        scratch_shapes=[
            pltpu.VMEM(((tok + KW - 1) * ch, LANES), F32), flat, flat, flat, flat, flat,
            pltpu.VMEM((ns * ch, LANES), F32),
            pltpu.VMEM((KW * ch, LANES), F32),
            pltpu.VMEM((tok * 2 * ns, LANES), F32),
            pltpu.VMEM((n_ten, 2 * ns, tok), F32),
            pltpu.VMEM((n_ctx, ch, LANES), F32),
            pltpu.VMEM((n_ctx, pieces, LANES), link),
            pltpu.VMEM((n_ctx, pieces, LANES), link),
            pltpu.VMEM((n_ctx, pieces, LANES), link),
            pltpu.VMEM((n_ctx, pieces, LANES), link),
            pltpu.VMEM((ns * ch, LANES), F32),
            pltpu.VMEM((n_ctx, tok, HEAD_WIDTH), BF16),
            pltpu.VMEM((n_ctx, tok, HEAD_WIDTH), BF16),
            pltpu.VMEM((n_ctx, group, tok, tok), F32),
            pltpu.VMEM((group, tok, tok), F32),
            pltpu.VMEM((group, tok, tok), F32),
            pltpu.VMEM((group, tok, HEAD_WIDTH), F32),
            dma, dma, dma((n_ten,)), dma((n_ten,)),
        ] + [dma((n_ctx,))] * 10,
        compiler_params=pltpu.CompilerParams(
            collective_id=0, has_side_effects=True, vmem_limit_bytes=60 << 20
        ),
    )(
        length, mamba_in, gate_in, step_raw, conv_weight, conv_bias.reshape(ch, LANES),
        step_bias.reshape(ch, LANES), decay_rates, skip_gain.reshape(ch, LANES), state_proj,
        query_input_rows, key_input_rows, value_input_rows,
    )


def solution(mesh):
    both = P("context", "tensor")
    in_specs = (
        P(), both, both, both, P(None, "tensor"), P("tensor"), P("tensor"), P(None, "tensor"),
        P("tensor"), P("tensor", None), both, both, both,
    )
    body = functools.partial(shards, mesh.shape["context"], mesh.shape["tensor"])
    return jax.shard_map(body, mesh=mesh, in_specs=in_specs, out_specs=(both, both), check_vma=False)
```

```python
import functools
import math

import jax
import jax.numpy as jnp
from jax import lax
from jax.experimental import pallas as pl
from jax.experimental.pallas import tpu as pltpu
from jax.sharding import PartitionSpec as P

KW = 4
HEAD_WIDTH = 128
LANES = 128
LOG2E = 1.4426950408889634
LOW = -1e30
MESH = pl.DeviceIdType.MESH
F32 = jnp.float32
BF16 = jnp.bfloat16


def each(count, body):
    if count <= 8:
        for i in range(count):
            body(i)
    else:
        @pl.loop(0, count)
        def _(i):
            body(i)


def blocked(count, step, body, start=0):
    @pl.loop(start // step, count // step)
    def _(block):
        for k in range(step):
            body(block * step + k)


def silu(v):
    return v / (1.0 + jnp.exp(-v))


def kernel(
    n_ctx, n_ten, group,
    length, mamba_hbm, step_hbm, conv_w_hbm, step_b_hbm, rates_hbm, conv_b_hbm, proj_hbm, gate_hbm,
    keys_hbm, values_hbm, skip_hbm, query_hbm,
    mamba_out_hbm, attn_out_hbm,
    mamba, step_raw, conv_w, step_b, rates, conv_b, proj, gate, skip, query, mamba_out, attn_out,
    x_a, conv_a, step_a, elapsed_a, gate_a, y_a, rate_a, taps_a, spread,
    part_all, e_all, s_out, s_in, p_out, p_in, inc_a, kv_all, sc, top, tot, acc,
    halo_send, halo_recv, part_send, part_recv, e_send, e_recv, s_send, s_recv,
    p_send, p_recv, kv_send, kv_recv, kv_forward, load_sem, store_sem,
):
    tok, chans = mamba.shape
    ch = chans // LANES
    ns = rates.shape[0]
    pieces = ns * ch // n_ctx
    me = lax.axis_index("context")
    mt = lax.axis_index("tensor")

    def ctx_copy(src, dst, send, recv, to):
        return pltpu.make_async_remote_copy(
            src_ref=src, dst_ref=dst, send_sem=send, recv_sem=recv,
            device_id={"context": to}, device_id_type=MESH,
        )

    def others(body):
        each(n_ctx - 1, lambda d: body(lax.rem(me + d + 1, n_ctx)))

    barrier = pltpu.get_barrier_semaphore()
    others(lambda to: pl.semaphore_signal(barrier, inc=1, device_id={"context": to}, device_id_type=MESH))
    for d in range(1, n_ten):
        pl.semaphore_signal(
            barrier, inc=1, device_id={"tensor": lax.rem(mt + d, n_ten)}, device_id_type=MESH
        )

    sources = (
        mamba_hbm, step_hbm, conv_w_hbm, step_b_hbm, rates_hbm, conv_b_hbm, proj_hbm, gate_hbm,
        keys_hbm, values_hbm, skip_hbm, query_hbm,
    )
    targets = (
        mamba, step_raw, conv_w, step_b, rates, conv_b, proj, gate,
        kv_all.at[me, 0], kv_all.at[me, 1], skip, query,
    )
    loads = [
        pltpu.make_async_copy(src, dst, load_sem.at[i])
        for i, (src, dst) in enumerate(zip(sources, targets))
    ]
    for load in loads:
        load.start()

    prompt_end = length[0]
    first = me * tok
    valid = (first + lax.broadcasted_iota(jnp.int32, (tok, LANES), 0)) < prompt_end
    pad = (KW - 1) * ch
    for load in loads[:6]:
        load.wait()

    @pl.loop(0, ch)
    def _(c):
        lanes = pl.ds(pl.multiple_of(c * LANES, LANES), LANES)
        x_a[pl.ds(pad + c, tok, stride=ch), :] = mamba[:, lanes].astype(F32)
        raw = step_raw[:, lanes].astype(F32) + step_b[pl.ds(c, 1), :]
        size = jnp.maximum(raw, 0.0) + jnp.log(1.0 + jnp.exp(-jnp.abs(raw)))
        step_a[pl.ds(c, tok, stride=ch), :] = jnp.where(valid, size, 0.0)
        rate_a[pl.ds(c, ns, stride=ch), :] = rates[:, lanes] * (-LOG2E)
        for j in range(KW):
            taps_a[pl.ds(j * ch + c, 1), :] = conv_w[j : j + 1, lanes]

    def run_elapsed(i, total):
        for k in range(4):
            rows = pl.ds(pl.multiple_of((i * 4 + k) * ch, ch), ch)
            total = total + step_a[rows, :]
            elapsed_a[rows, :] = total
        return total

    e_all[me] = lax.fori_loop(0, tok // 4, run_elapsed, jnp.zeros((ch, LANES), F32))

    bias = conv_b[...]

    def convolve(t):
        total = bias
        for j in range(KW):
            total = total + taps_a[j * ch : (j + 1) * ch, :] * x_a[
                pl.ds(pl.multiple_of((t + j) * ch, ch), ch), :
            ]
        conv_a[pl.ds(pl.multiple_of(t * ch, ch), ch), :] = silu(total).astype(BF16).astype(F32)

    blocked(tok, 4, convolve, start=4)
    for load in loads[6:10]:
        load.wait()

    @pl.loop(0, ch)
    def _(c):
        lanes = pl.ds(pl.multiple_of(c * LANES, LANES), LANES)
        gate_a[pl.ds(c, tok, stride=ch), :] = silu(gate[:, lanes].astype(F32))

    pl.semaphore_wait(barrier, n_ctx - 1 + n_ten - 1)

    halo = ctx_copy(
        x_a.at[pl.ds(tok * ch, pad), :], x_a.at[pl.ds(0, pad), :],
        halo_send, halo_recv, lax.rem(me + 1, n_ctx),
    )

    @pl.when(me < n_ctx - 1)
    def _():
        halo.start()

    twin = me + 1 - 2 * lax.rem(me, 2)

    def kv_copy(src, to, send):
        return ctx_copy(kv_all.at[src], kv_all.at[src], send, kv_recv.at[src], to)

    def kv_line(body):
        def visit(d):
            to = me + 2 * (d + 1)

            @pl.when(to < n_ctx)
            def _():
                body(to)

        each(n_ctx // 2 - 1, visit)

        @pl.when(lax.rem(me, 2) == 0)
        def _():
            body(me + 1)

    kv_line(lambda to: kv_copy(me, to, kv_send.at[to]).start())

    def forward(lo, hi):
        def visit(d):
            src = me - 2 * (d + 1 + lo)

            @pl.when(src >= 0)
            def _():
                kv_copy(src, twin, kv_forward.at[src]).wait_recv()
                kv_copy(src, twin, kv_forward.at[src]).start()

        each(hi - lo, visit)

    def e_copy(src, to):
        return ctx_copy(e_all.at[src], e_all.at[src], e_send.at[to], e_recv.at[src], to)

    others(lambda to: e_copy(me, to).start())


    @pl.when(me > 0)
    def _():
        halo.wait_recv()

    @pl.when(me == 0)
    def _():
        x_a[0:pad, :] = jnp.zeros((pad, LANES), F32)

    for t in range(4):
        convolve(t)

    part = jnp.zeros((2 * ns, tok), F32)
    for c in range(ch):
        part = part + lax.dot_general(
            proj[:, c * LANES : (c + 1) * LANES],
            conv_a[pl.ds(c, tok, stride=ch), :].astype(BF16),
            (((1,), (1,)), ((), ())),
            preferred_element_type=F32,
        )
    part_all[mt] = part

    def part_copy(src, to):
        return pltpu.make_async_remote_copy(
            src_ref=part_all.at[src], dst_ref=part_all.at[src],
            send_sem=part_send.at[to], recv_sem=part_recv.at[src],
            device_id={"tensor": to}, device_id_type=MESH,
        )

    for d in range(1, n_ten):
        part_copy(mt, lax.rem(mt + d, n_ten)).start()
    steps = n_ctx // 2 - 1
    forward(0, 1)

    for d in range(1, n_ten):
        part_copy(lax.rem(mt + d, n_ten), mt).wait_recv()
    projected = part_all[0]
    for d in range(1, n_ten):
        projected = projected + part_all[d]
    projected = projected.T
    for n in range(2 * ns):
        spread[pl.ds(n, tok, stride=2 * ns), :] = jnp.broadcast_to(
            projected[:, n : n + 1], (tok, LANES)
        )

    forward(1, 2)
    for load in loads[10:]:
        load.wait()
    skip_now = skip[...]

    def advance(t, states):
        rows = pl.ds(pl.multiple_of(t * ch, ch), ch)
        size = step_a[rows, :]
        mixed = conv_a[rows, :]
        driven = size * mixed
        sums = [skip_now * mixed, None]
        new = []
        for n in range(ns):
            decay = jnp.exp2(rate_a[n * ch : (n + 1) * ch, :] * size)
            inject = jnp.broadcast_to(spread[pl.ds(t * 2 * ns + n, 1), :], (ch, LANES))
            readout = jnp.broadcast_to(spread[pl.ds(t * 2 * ns + ns + n, 1), :], (ch, LANES))
            state = decay * states[n] + inject * driven
            new.append(state)
            term = readout * state
            sums[n % 2] = term if sums[n % 2] is None else sums[n % 2] + term
        y_a[rows, :] = sums[0] + sums[1]
        return tuple(new)

    finals = lax.fori_loop(
        0, tok // 2, advance, tuple(jnp.zeros((ch, LANES), F32) for _ in range(ns))
    )
    forward(2, steps)
    finals = lax.fori_loop(tok // 2, tok, advance, finals)
    whole_state = jnp.concatenate(finals, axis=0).astype(s_out.dtype)
    s_out[...] = whole_state.reshape(n_ctx, pieces, LANES)

    def s_copy(src, to):
        return ctx_copy(s_out.at[to], s_in.at[src], s_send.at[to], s_recv.at[src], to)

    others(lambda to: s_copy(me, to).start())
    s_in[me] = s_out[me]

    def arrive(d):
        src = twin - 2 * (d + 1)

        @pl.when(src >= 0)
        def _():
            kv_copy(src, twin, kv_send.at[src]).wait_recv()

    each(steps, arrive)

    @pl.when(lax.rem(me, 2) == 1)
    def _():
        kv_copy(me - 1, twin, kv_send.at[0]).wait_recv()

    scale = LOG2E / math.sqrt(HEAD_WIDTH)
    heads = query.shape[1] // HEAD_WIDTH
    row_pos = first + lax.broadcasted_iota(jnp.int32, (tok, tok), 0)
    last_key = jnp.minimum(row_pos, prompt_end - 1)
    key_iota = lax.broadcasted_iota(jnp.int32, (tok, tok), 1)

    def attend(head0):
        top[...] = jnp.full(top.shape, LOW, F32)
        tot[...] = jnp.zeros(tot.shape, F32)
        acc[...] = jnp.zeros(acc.shape, F32)

        @pl.loop(0, me + 1)
        def _(j):
            block = kv_all[j, 0]
            allowed = (key_iota + j * tok) <= last_key
            for g in range(group):
                cols = slice((head0 + g) * HEAD_WIDTH, (head0 + g + 1) * HEAD_WIDTH)
                s = lax.dot_general(
                    query[:, cols], block, (((1,), (1,)), ((), ())), preferred_element_type=F32
                )
                s = jnp.where(allowed, s, LOW)
                top[g] = jnp.maximum(top[g], s)
                sc[j, g] = s

        highest = [jnp.max(top[g], axis=1, keepdims=True) for g in range(group)]
        for g in range(group):
            top[g] = jnp.broadcast_to(highest[g], (tok, tok))

        @pl.loop(0, me + 1)
        def _(j):
            block = kv_all[j, 1]
            for g in range(group):
                w = jnp.exp2((sc[j, g] - top[g]) * scale)
                tot[g] = tot[g] + w
                acc[g] = acc[g] + jnp.dot(w.astype(BF16), block, preferred_element_type=F32)

        for g in range(group):
            cols = slice((head0 + g) * HEAD_WIDTH, (head0 + g + 1) * HEAD_WIDTH)
            total = jnp.sum(tot[g], axis=1, keepdims=True)
            attn_out[:, cols] = (acc[g] / total).astype(BF16)

    starts = list(range(0, heads, group))
    half = len(starts) // 2
    for head0 in starts[:half]:
        attend(head0)

    others(lambda src: e_copy(src, me).wait_recv())
    others(lambda src: s_copy(src, me).wait_recv())
    my_rate = rate_a[pl.ds(me * pieces, pieces), :]

    def fold(j, running):
        p_out[j] = running.astype(p_out.dtype)
        if pieces >= ch:
            gone = jnp.concatenate([e_all[j]] * (pieces // ch), axis=0)
        else:
            gone = e_all[j, pl.ds(lax.rem(me * pieces, ch), pieces), :]
        return jnp.exp2(my_rate * gone) * running + s_in[j].astype(F32)

    lax.fori_loop(0, n_ctx, fold, jnp.zeros((pieces, LANES), F32))

    def p_copy(src, to):
        return ctx_copy(p_out.at[to], p_in.at[src], p_send.at[to], p_recv.at[src], to)

    others(lambda to: p_copy(me, to).start())
    p_in[me] = p_out[me]

    for head0 in starts[half:]:
        attend(head0)

    others(lambda src: p_copy(src, me).wait_recv())
    inc_a[...] = p_in[...].reshape(ns * ch, LANES).astype(F32)

    def correct(t):
        rows = pl.ds(pl.multiple_of(t * ch, ch), ch)
        gone = elapsed_a[rows, :]
        sums = [y_a[rows, :], None]
        for n in range(ns):
            held = jnp.exp2(rate_a[n * ch : (n + 1) * ch, :] * gone) * inc_a[n * ch : (n + 1) * ch, :]
            term = jnp.broadcast_to(spread[pl.ds(t * 2 * ns + ns + n, 1), :], (ch, LANES)) * held
            sums[n % 2] = term if sums[n % 2] is None else sums[n % 2] + term
        y_a[rows, :] = (sums[0] + sums[1]) * gate_a[rows, :]

    store = pltpu.make_async_copy(attn_out, attn_out_hbm, store_sem.at[0])
    store.start()
    blocked(tok, 2, correct)

    @pl.loop(0, ch)
    def _(c):
        lanes = pl.ds(pl.multiple_of(c * LANES, LANES), LANES)
        mamba_out[:, lanes] = y_a[pl.ds(c, tok, stride=ch), :].astype(BF16)

    @pl.when(me < n_ctx - 1)
    def _():
        halo.wait_send()

    out = pltpu.make_async_copy(mamba_out, mamba_out_hbm, store_sem.at[1])
    out.start()
    kv_line(lambda to: kv_copy(me, to, kv_send.at[to]).wait_send())

    def end_forward(d):
        src = me - 2 * (d + 1)

        @pl.when(src >= 0)
        def _():
            kv_copy(src, twin, kv_forward.at[src]).wait_send()

    each(steps, end_forward)
    others(lambda to: e_copy(me, to).wait_send())
    others(lambda to: s_copy(me, to).wait_send())
    others(lambda to: p_copy(me, to).wait_send())
    for d in range(1, n_ten):
        part_copy(mt, lax.rem(mt + d, n_ten)).wait_send()
    store.wait()
    out.wait()


def shards(
    n_ctx, n_ten,
    length, mamba_in, gate_in, step_raw, conv_weight, conv_bias, step_bias, decay_rates, skip_gain,
    state_proj, query_input_rows, key_input_rows, value_input_rows,
):
    tok, chans = mamba_in.shape
    ch = chans // LANES
    ns = decay_rates.shape[0]
    heads = query_input_rows.shape[1] // HEAD_WIDTH
    group = heads // 2
    while group > 1 and n_ctx * group * tok * tok * 4 > (17 << 20):
        group //= 2
    pieces = ns * ch // n_ctx
    link = BF16 if pieces % 16 == 0 else F32
    dma = pltpu.SemaphoreType.DMA
    flat = pltpu.VMEM((tok * ch, LANES), F32)
    hbm = pl.BlockSpec(memory_space=pl.ANY)
    ordered = (
        mamba_in, step_raw, conv_weight, step_bias.reshape(ch, LANES), decay_rates,
        conv_bias.reshape(ch, LANES), state_proj.T, gate_in, key_input_rows, value_input_rows,
        skip_gain.reshape(ch, LANES), query_input_rows,
    )
    held = [pltpu.VMEM(a.shape, a.dtype) for i, a in enumerate(ordered) if i not in (8, 9)]
    return pl.pallas_call(
        functools.partial(kernel, n_ctx, n_ten, group),
        out_shape=(
            jax.ShapeDtypeStruct(mamba_in.shape, BF16),
            jax.ShapeDtypeStruct(query_input_rows.shape, BF16),
        ),
        in_specs=[pl.BlockSpec(memory_space=pltpu.SMEM)] + [hbm] * 12,
        out_specs=(hbm, hbm),
        scratch_shapes=held + [
            pltpu.VMEM(mamba_in.shape, BF16),
            pltpu.VMEM(query_input_rows.shape, BF16),
            pltpu.VMEM(((tok + KW - 1) * ch, LANES), F32), flat, flat, flat, flat, flat,
            pltpu.VMEM((ns * ch, LANES), F32),
            pltpu.VMEM((KW * ch, LANES), F32),
            pltpu.VMEM((tok * 2 * ns, LANES), F32),
            pltpu.VMEM((n_ten, 2 * ns, tok), F32),
            pltpu.VMEM((n_ctx, ch, LANES), F32),
            pltpu.VMEM((n_ctx, pieces, LANES), link),
            pltpu.VMEM((n_ctx, pieces, LANES), link),
            pltpu.VMEM((n_ctx, pieces, LANES), link),
            pltpu.VMEM((n_ctx, pieces, LANES), link),
            pltpu.VMEM((ns * ch, LANES), F32),
            pltpu.VMEM((n_ctx, 2, tok, HEAD_WIDTH), BF16),
            pltpu.VMEM((n_ctx, group, tok, tok), F32),
            pltpu.VMEM((group, tok, tok), F32),
            pltpu.VMEM((group, tok, tok), F32),
            pltpu.VMEM((group, tok, HEAD_WIDTH), F32),
            dma, dma, dma((n_ten,)), dma((n_ten,)),
        ] + [dma((n_ctx,))] * 9 + [dma((len(ordered),)), dma((2,))],
        compiler_params=pltpu.CompilerParams(
            collective_id=0, has_side_effects=True, vmem_limit_bytes=60 << 20
        ),
    )(length, *ordered)


def solution(mesh):
    both = P("context", "tensor")
    in_specs = (
        P(), both, both, both, P(None, "tensor"), P("tensor"), P("tensor"), P(None, "tensor"),
        P("tensor"), P("tensor", None), both, both, both,
    )
    body = functools.partial(shards, mesh.shape["context"], mesh.shape["tensor"])
    return jax.shard_map(body, mesh=mesh, in_specs=in_specs, out_specs=(both, both), check_vma=False)
```

```python
import functools
import math

import jax
import jax.numpy as jnp
from jax import lax
from jax.experimental import pallas as pl
from jax.experimental.pallas import tpu as pltpu
from jax.sharding import PartitionSpec as P

KW = 4
HEAD_WIDTH = 128
LANES = 128
LOG2E = 1.4426950408889634
LOW = -1e30
MESH = pl.DeviceIdType.MESH
F32 = jnp.float32
BF16 = jnp.bfloat16


def each(count, body):
    if count <= 8:
        for i in range(count):
            body(i)
    else:
        @pl.loop(0, count)
        def _(i):
            body(i)


def blocked(count, step, body, start=0):
    @pl.loop(start // step, count // step)
    def _(block):
        for k in range(step):
            body(block * step + k)


def silu(v):
    return v / (1.0 + jnp.exp(-v))


def kernel(
    n_ctx, n_ten, group,
    length, mamba_hbm, step_hbm, conv_w_hbm, step_b_hbm, rates_hbm, conv_b_hbm, proj_hbm, gate_hbm,
    keys_hbm, values_hbm, skip_hbm, query_hbm,
    mamba_out_hbm, attn_out_hbm,
    mamba, step_raw, conv_w, step_b, rates, conv_b, proj, gate, skip, query, mamba_out, attn_out,
    x_a, conv_a, step_a, elapsed_a, gate_a, y_a, rate_a, taps_a, spread,
    part_all, e_all, s_out, s_in, p_out, p_in, inc_a, kv_all, sc, top, tot, acc,
    halo_send, halo_recv, part_send, part_recv, s_send, s_recv, p_send, p_recv, e_send, e_recv,
    kv_send, kv_recv, kv_forward, load_sem, store_sem,
):
    tok, chans = mamba.shape
    ch = chans // LANES
    ns = rates.shape[0]
    hh = ch // 2
    pieces = ns * hh // n_ctx
    me = lax.axis_index("context")
    mt = lax.axis_index("tensor")

    def ctx_copy(src, dst, send, recv, to):
        return pltpu.make_async_remote_copy(
            src_ref=src, dst_ref=dst, send_sem=send, recv_sem=recv,
            device_id={"context": to}, device_id_type=MESH,
        )

    def others(body):
        each(n_ctx - 1, lambda d: body(lax.rem(me + d + 1, n_ctx)))

    barrier = pltpu.get_barrier_semaphore()
    others(lambda to: pl.semaphore_signal(barrier, inc=1, device_id={"context": to}, device_id_type=MESH))
    for d in range(1, n_ten):
        pl.semaphore_signal(
            barrier, inc=1, device_id={"tensor": lax.rem(mt + d, n_ten)}, device_id_type=MESH
        )

    sources = (
        mamba_hbm, step_hbm, conv_w_hbm, step_b_hbm, rates_hbm, conv_b_hbm, proj_hbm, gate_hbm,
        keys_hbm, values_hbm, skip_hbm, query_hbm,
    )
    targets = (
        mamba, step_raw, conv_w, step_b, rates, conv_b, proj, gate,
        kv_all.at[me, 0], kv_all.at[me, 1], skip, query,
    )
    loads = [
        pltpu.make_async_copy(src, dst, load_sem.at[i])
        for i, (src, dst) in enumerate(zip(sources, targets))
    ]
    for load in loads:
        load.start()

    prompt_end = length[0]
    first = me * tok
    valid = (first + lax.broadcasted_iota(jnp.int32, (tok, LANES), 0)) < prompt_end
    pad = (KW - 1) * ch
    for load in loads[:6]:
        load.wait()

    @pl.loop(0, ch)
    def _(c):
        lanes = pl.ds(pl.multiple_of(c * LANES, LANES), LANES)
        x_a[pl.ds(pad + c, tok, stride=ch), :] = mamba[:, lanes].astype(F32)
        raw = step_raw[:, lanes].astype(F32) + step_b[pl.ds(c, 1), :]
        size = jnp.maximum(raw, 0.0) + jnp.log(1.0 + jnp.exp(-jnp.abs(raw)))
        step_a[pl.ds(c, tok, stride=ch), :] = jnp.where(valid, size, 0.0)
        rate_a[pl.ds((c // hh) * (ns * hh) + c % hh, ns, stride=hh), :] = rates[:, lanes] * (-LOG2E)
        for j in range(KW):
            taps_a[pl.ds(j * ch + c, 1), :] = conv_w[j : j + 1, lanes]

    def run_elapsed(i, total):
        for k in range(4):
            rows = pl.ds(pl.multiple_of((i * 4 + k) * ch, ch), ch)
            total = total + step_a[rows, :]
            elapsed_a[rows, :] = total
        return total

    e_all[me] = lax.fori_loop(0, tok // 4, run_elapsed, jnp.zeros((ch, LANES), F32))

    bias = conv_b[...]

    def convolve(t):
        total = bias
        for j in range(KW):
            total = total + taps_a[j * ch : (j + 1) * ch, :] * x_a[
                pl.ds(pl.multiple_of((t + j) * ch, ch), ch), :
            ]
        conv_a[pl.ds(pl.multiple_of(t * ch, ch), ch), :] = silu(total).astype(BF16).astype(F32)

    blocked(tok, 4, convolve, start=4)
    for load in loads[6:10]:
        load.wait()

    @pl.loop(0, ch)
    def _(c):
        lanes = pl.ds(pl.multiple_of(c * LANES, LANES), LANES)
        gate_a[pl.ds(c, tok, stride=ch), :] = silu(gate[:, lanes].astype(F32))

    pl.semaphore_wait(barrier, n_ctx - 1 + n_ten - 1)

    halo = ctx_copy(
        x_a.at[pl.ds(tok * ch, pad), :], x_a.at[pl.ds(0, pad), :],
        halo_send, halo_recv, lax.rem(me + 1, n_ctx),
    )

    @pl.when(me < n_ctx - 1)
    def _():
        halo.start()

    twin = me + 1 - 2 * lax.rem(me, 2)

    def kv_copy(src, to, send):
        return ctx_copy(kv_all.at[src], kv_all.at[src], send, kv_recv.at[src], to)

    def kv_line(body):
        def visit(d):
            to = me + 2 * (d + 1)

            @pl.when(to < n_ctx)
            def _():
                body(to)

        each(n_ctx // 2 - 1, visit)

        @pl.when(lax.rem(me, 2) == 0)
        def _():
            body(me + 1)

    kv_line(lambda to: kv_copy(me, to, kv_send.at[to]).start())

    def forward(lo, hi):
        def visit(d):
            src = me - 2 * (d + 1 + lo)

            @pl.when(src >= 0)
            def _():
                kv_copy(src, twin, kv_forward.at[src]).wait_recv()
                kv_copy(src, twin, kv_forward.at[src]).start()

        each(hi - lo, visit)

    def e_copy(src, to):
        return ctx_copy(e_all.at[src], e_all.at[src], e_send.at[to], e_recv.at[src], to)

    others(lambda to: e_copy(me, to).start())


    @pl.when(me > 0)
    def _():
        halo.wait_recv()

    @pl.when(me == 0)
    def _():
        x_a[0:pad, :] = jnp.zeros((pad, LANES), F32)

    for t in range(4):
        convolve(t)

    part = jnp.zeros((2 * ns, tok), F32)
    for c in range(ch):
        part = part + lax.dot_general(
            proj[:, c * LANES : (c + 1) * LANES],
            conv_a[pl.ds(c, tok, stride=ch), :].astype(BF16),
            (((1,), (1,)), ((), ())),
            preferred_element_type=F32,
        )
    part_all[mt] = part

    def part_copy(src, to):
        return pltpu.make_async_remote_copy(
            src_ref=part_all.at[src], dst_ref=part_all.at[src],
            send_sem=part_send.at[to], recv_sem=part_recv.at[src],
            device_id={"tensor": to}, device_id_type=MESH,
        )

    for d in range(1, n_ten):
        part_copy(mt, lax.rem(mt + d, n_ten)).start()
    steps = n_ctx // 2 - 1
    forward(0, 1)

    for d in range(1, n_ten):
        part_copy(lax.rem(mt + d, n_ten), mt).wait_recv()
    projected = part_all[0]
    for d in range(1, n_ten):
        projected = projected + part_all[d]
    projected = projected.T
    for n in range(2 * ns):
        spread[pl.ds(n, tok, stride=2 * ns), :] = jnp.broadcast_to(
            projected[:, n : n + 1], (tok, LANES)
        )

    forward(1, 2)
    for load in loads[10:]:
        load.wait()
    def s_copy(part, src, to):
        return ctx_copy(
            s_out.at[part, to], s_in.at[part, src],
            s_send.at[part, to], s_recv.at[part, src], to,
        )

    def p_copy(part, src, to):
        return ctx_copy(
            p_out.at[part, to], p_in.at[part, src],
            p_send.at[part, to], p_recv.at[part, src], to,
        )

    def scan(part):
        base = part * ns * hh
        skip_now = skip[part * hh : (part + 1) * hh, :]

        def advance(t, states):
            rows = pl.ds(pl.multiple_of(t * ch + part * hh, hh), hh)
            size = step_a[rows, :]
            mixed = conv_a[rows, :]
            driven = size * mixed
            sums = [skip_now * mixed, None]
            new = []
            for n in range(ns):
                decay = jnp.exp2(rate_a[base + n * hh : base + (n + 1) * hh, :] * size)
                inject = jnp.broadcast_to(spread[pl.ds(t * 2 * ns + n, 1), :], (hh, LANES))
                readout = jnp.broadcast_to(spread[pl.ds(t * 2 * ns + ns + n, 1), :], (hh, LANES))
                state = decay * states[n] + inject * driven
                new.append(state)
                term = readout * state
                sums[n % 2] = term if sums[n % 2] is None else sums[n % 2] + term
            y_a[rows, :] = sums[0] + sums[1]
            return tuple(new)

        def advance_block(block, states):
            for k in range(4):
                states = advance(block * 4 + k, states)
            return states

        finals = lax.fori_loop(
            0, tok // 4, advance_block, tuple(jnp.zeros((hh, LANES), F32) for _ in range(ns))
        )
        whole_state = jnp.concatenate(finals, axis=0).astype(s_out.dtype)
        s_out[part] = whole_state.reshape(n_ctx, pieces, LANES)
        others(lambda to: s_copy(part, me, to).start())
        s_in[part, me] = s_out[part, me]

    def fold_part(part):
        others(lambda src: s_copy(part, src, me).wait_recv())
        my_rate = rate_a[pl.ds(part * ns * hh + me * pieces, pieces), :]

        def fold(j, running):
            p_out[part, j] = running.astype(p_out.dtype)
            if pieces >= hh:
                gone = jnp.concatenate(
                    [e_all[j, part * hh : (part + 1) * hh, :]] * (pieces // hh), axis=0
                )
            else:
                gone = e_all[j, pl.ds(part * hh + lax.rem(me * pieces, hh), pieces), :]
            return jnp.exp2(my_rate * gone) * running + s_in[part, j].astype(F32)

        lax.fori_loop(0, n_ctx, fold, jnp.zeros((pieces, LANES), F32))
        others(lambda to: p_copy(part, me, to).start())
        p_in[part, me] = p_out[part, me]

    def correct_part(part):
        base = part * ns * hh
        others(lambda src: p_copy(part, src, me).wait_recv())
        inc_a[base : base + ns * hh, :] = p_in[part].reshape(ns * hh, LANES).astype(F32)

        def correct(t):
            rows = pl.ds(pl.multiple_of(t * ch + part * hh, hh), hh)
            gone = elapsed_a[rows, :]
            sums = [y_a[rows, :], None]
            for n in range(ns):
                span = slice(base + n * hh, base + (n + 1) * hh)
                held = jnp.exp2(rate_a[span, :] * gone) * inc_a[span, :]
                term = jnp.broadcast_to(spread[pl.ds(t * 2 * ns + ns + n, 1), :], (hh, LANES)) * held
                sums[n % 2] = term if sums[n % 2] is None else sums[n % 2] + term
            y_a[rows, :] = (sums[0] + sums[1]) * gate_a[rows, :]

        blocked(tok, 4, correct)

    scan(0)
    forward(2, steps)
    scan(1)
    others(lambda src: e_copy(src, me).wait_recv())
    fold_part(0)

    def arrive(d):
        src = twin - 2 * (d + 1)

        @pl.when(src >= 0)
        def _():
            kv_copy(src, twin, kv_send.at[src]).wait_recv()

    each(steps, arrive)

    @pl.when(lax.rem(me, 2) == 1)
    def _():
        kv_copy(me - 1, twin, kv_send.at[0]).wait_recv()

    scale = LOG2E / math.sqrt(HEAD_WIDTH)
    heads = query.shape[1] // HEAD_WIDTH
    row_pos = first + lax.broadcasted_iota(jnp.int32, (tok, tok), 0)
    last_key = jnp.minimum(row_pos, prompt_end - 1)
    key_iota = lax.broadcasted_iota(jnp.int32, (tok, tok), 1)

    def attend(head0):
        top[...] = jnp.full(top.shape, LOW, F32)
        tot[...] = jnp.zeros(tot.shape, F32)
        acc[...] = jnp.zeros(acc.shape, F32)

        @pl.loop(0, me + 1)
        def _(j):
            block = kv_all[j, 0]
            allowed = (key_iota + j * tok) <= last_key
            for g in range(group):
                cols = slice((head0 + g) * HEAD_WIDTH, (head0 + g + 1) * HEAD_WIDTH)
                s = lax.dot_general(
                    query[:, cols], block, (((1,), (1,)), ((), ())), preferred_element_type=F32
                )
                s = jnp.where(allowed, s, LOW)
                top[g] = jnp.maximum(top[g], s)
                sc[j, g] = s

        highest = [jnp.max(top[g], axis=1, keepdims=True) for g in range(group)]
        for g in range(group):
            top[g] = jnp.broadcast_to(highest[g], (tok, tok))

        @pl.loop(0, me + 1)
        def _(j):
            block = kv_all[j, 1]
            for g in range(group):
                w = jnp.exp2((sc[j, g] - top[g]) * scale)
                tot[g] = tot[g] + w
                acc[g] = acc[g] + jnp.dot(w.astype(BF16), block, preferred_element_type=F32)

        for g in range(group):
            cols = slice((head0 + g) * HEAD_WIDTH, (head0 + g + 1) * HEAD_WIDTH)
            total = jnp.sum(tot[g], axis=1, keepdims=True)
            attn_out[:, cols] = (acc[g] / total).astype(BF16)

    starts = list(range(0, heads, group))
    half = len(starts) // 2
    for head0 in starts[:half]:
        attend(head0)

    fold_part(1)

    for head0 in starts[half:]:
        attend(head0)

    store = pltpu.make_async_copy(attn_out, attn_out_hbm, store_sem.at[0])
    store.start()
    correct_part(0)
    correct_part(1)

    @pl.loop(0, ch)
    def _(c):
        lanes = pl.ds(pl.multiple_of(c * LANES, LANES), LANES)
        mamba_out[:, lanes] = y_a[pl.ds(c, tok, stride=ch), :].astype(BF16)

    @pl.when(me < n_ctx - 1)
    def _():
        halo.wait_send()

    out = pltpu.make_async_copy(mamba_out, mamba_out_hbm, store_sem.at[1])
    out.start()
    kv_line(lambda to: kv_copy(me, to, kv_send.at[to]).wait_send())

    def end_forward(d):
        src = me - 2 * (d + 1)

        @pl.when(src >= 0)
        def _():
            kv_copy(src, twin, kv_forward.at[src]).wait_send()

    each(steps, end_forward)
    others(lambda to: e_copy(me, to).wait_send())
    for part in range(2):
        others(lambda to: s_copy(part, me, to).wait_send())
        others(lambda to: p_copy(part, me, to).wait_send())
    for d in range(1, n_ten):
        part_copy(mt, lax.rem(mt + d, n_ten)).wait_send()
    store.wait()
    out.wait()


def shards(
    n_ctx, n_ten,
    length, mamba_in, gate_in, step_raw, conv_weight, conv_bias, step_bias, decay_rates, skip_gain,
    state_proj, query_input_rows, key_input_rows, value_input_rows,
):
    tok, chans = mamba_in.shape
    ch = chans // LANES
    ns = decay_rates.shape[0]
    heads = query_input_rows.shape[1] // HEAD_WIDTH
    group = heads // 2
    while group > 1 and n_ctx * group * tok * tok * 4 > (17 << 20):
        group //= 2
    pieces = ns * ch // 2 // n_ctx
    link = BF16 if pieces % 16 == 0 else F32
    dma = pltpu.SemaphoreType.DMA
    flat = pltpu.VMEM((tok * ch, LANES), F32)
    hbm = pl.BlockSpec(memory_space=pl.ANY)
    ordered = (
        mamba_in, step_raw, conv_weight, step_bias.reshape(ch, LANES), decay_rates,
        conv_bias.reshape(ch, LANES), state_proj.T, gate_in, key_input_rows, value_input_rows,
        skip_gain.reshape(ch, LANES), query_input_rows,
    )
    held = [pltpu.VMEM(a.shape, a.dtype) for i, a in enumerate(ordered) if i not in (8, 9)]
    return pl.pallas_call(
        functools.partial(kernel, n_ctx, n_ten, group),
        out_shape=(
            jax.ShapeDtypeStruct(mamba_in.shape, BF16),
            jax.ShapeDtypeStruct(query_input_rows.shape, BF16),
        ),
        in_specs=[pl.BlockSpec(memory_space=pltpu.SMEM)] + [hbm] * 12,
        out_specs=(hbm, hbm),
        scratch_shapes=held + [
            pltpu.VMEM(mamba_in.shape, BF16),
            pltpu.VMEM(query_input_rows.shape, BF16),
            pltpu.VMEM(((tok + KW - 1) * ch, LANES), F32), flat, flat, flat, flat, flat,
            pltpu.VMEM((ns * ch, LANES), F32),
            pltpu.VMEM((KW * ch, LANES), F32),
            pltpu.VMEM((tok * 2 * ns, LANES), F32),
            pltpu.VMEM((n_ten, 2 * ns, tok), F32),
            pltpu.VMEM((n_ctx, ch, LANES), F32),
            pltpu.VMEM((2, n_ctx, pieces, LANES), link),
            pltpu.VMEM((2, n_ctx, pieces, LANES), link),
            pltpu.VMEM((2, n_ctx, pieces, LANES), link),
            pltpu.VMEM((2, n_ctx, pieces, LANES), link),
            pltpu.VMEM((ns * ch, LANES), F32),
            pltpu.VMEM((n_ctx, 2, tok, HEAD_WIDTH), BF16),
            pltpu.VMEM((n_ctx, group, tok, tok), F32),
            pltpu.VMEM((group, tok, tok), F32),
            pltpu.VMEM((group, tok, tok), F32),
            pltpu.VMEM((group, tok, HEAD_WIDTH), F32),
            dma, dma, dma((n_ten,)), dma((n_ten,)),
        ] + [dma((2, n_ctx))] * 4 + [dma((n_ctx,))] * 5 + [dma((len(ordered),)), dma((2,))],
        compiler_params=pltpu.CompilerParams(
            collective_id=0, has_side_effects=True, vmem_limit_bytes=60 << 20
        ),
    )(length, *ordered)


def solution(mesh):
    both = P("context", "tensor")
    in_specs = (
        P(), both, both, both, P(None, "tensor"), P("tensor"), P("tensor"), P(None, "tensor"),
        P("tensor"), P("tensor", None), both, both, both,
    )
    body = functools.partial(shards, mesh.shape["context"], mesh.shape["tensor"])
    return jax.shard_map(body, mesh=mesh, in_specs=in_specs, out_specs=(both, both), check_vma=False)
```
